256 devices in a mesh: row: 16 (over z, core), col: 16 (over x, y).
Axes of the slice: x: 4, y: 4, z: 8, core: 2. Of those that a mesh axis runs over, the one named last changes fastest.
Arguments:
- diag_rows: bfloat16 [16, 256, 512, 512], P('row', 'col'), may hold values from -0.12988281 to 0.12988281
- next_rows: bfloat16 [16, 256, 128, 512], P('row', 'col'), may hold values from -6 to 6
- routes: int32 [16, 16, 16], P('row', 'col'), may hold values from 0 to 15, each once within a row
- diag_blocks: bfloat16 [16, 16, 512, 512], P('row', 'col'), as said below
- panel_blocks: bfloat16 [16, 16, 128, 512], P('row', 'col'), may hold values from -6 to 6
Outputs:
- diag_factor: bfloat16 [16, 16, 512, 512], P('row', 'col')
- panel_factor: bfloat16 [16, 16, 128, 512], P('row', 'col')
The draws below stay inside these ranges and needn't reach their ends.
Inputs may be any that keep to these rules, and one draw needn't show every extreme that they name: `routes`: the 16 sources of one device name every target column exactly once. `diag_blocks`: every block is symmetric positive definite with eigenvalues of at least 0.5 before rounding.
All inputs are finite; a program needn't handle non-finite values.
Results may differ from the reference program's by a relative error of at most 0.001.
Values may be sent and summed in bfloat16 or wider, within the bound.
No kernel may reach another device: no remote copies, remote signals or barrier semaphores. Data moves between devices by JAX's collectives and lax.ppermute only.
A program may use at most 128 MiB of HBM per device.

```python
import jax
import jax.numpy as jnp
from jax import lax

BS = 512
RB = 128
PROWS = 16
PCOLS = 16
KD = 16


def draw_diag_blocks(key, part):
    key_rows, key_shift = jax.random.split(key, 2)
    raw_rows = jax.random.normal(key_rows, (PROWS, PCOLS, BS, BS), jnp.float32)
    gram_part = jnp.einsum('gcik,gcjk->gcij', raw_rows, raw_rows) / BS
    diag_shift = jax.random.uniform(key_shift, (PROWS, PCOLS, BS), jnp.float32, 0.5, 2.0)
    return (gram_part + diag_shift[..., None] * jnp.eye(BS, dtype=jnp.float32)).astype(jnp.bfloat16)


def levels(own_key, dims, cuts, smallest, largest):
    gain = 1.0
    for position, shards_of in cuts:
        draws = jax.random.uniform(jax.random.fold_in(jax.random.fold_in(own_key, 6), position), (shards_of,), jnp.float32, smallest / len(cuts), largest / len(cuts))
        gain = gain * jnp.repeat(jnp.exp(draws), dims[position] // shards_of).reshape((-1,) + (1,) * (len(dims) - 1 - position))
    return gain


def noise(key, shape, scale, reach, cuts=(), kind=jnp.bfloat16):
    values = scale * jax.random.normal(key, shape, jnp.float32)
    if cuts:
        values = values * levels(key, shape, cuts, -0.22, 0.18)
    return jnp.clip(values, -reach, reach).astype(kind)


def setup_inputs(seed: int = 0) -> dict:
    arg_keys = jax.random.split(jax.random.key(seed), 6)
    return {
        "diag_rows": noise(arg_keys[0], (PROWS, PCOLS * KD, BS, BS), 0.022, 0.12988281, ((0, 16), (1, 16))),
        "next_rows": noise(arg_keys[1], (PROWS, PCOLS * KD, RB, BS), 1.0, 6.0, ((0, 16), (1, 16))),
        "routes": jax.vmap(lambda own: jax.random.permutation(own, PCOLS))(jax.random.split(arg_keys[2], PROWS * PCOLS)).reshape((PROWS, PCOLS, KD)).astype(jnp.int32),
        "diag_blocks": draw_diag_blocks(jax.random.fold_in(arg_keys[5], 71), 0),
        "panel_blocks": noise(arg_keys[4], (PROWS, PCOLS, RB, BS), 1.0, 6.0, ((0, 16), (1, 16))),
    }


def reference(diag_rows, next_rows, routes, diag_blocks, panel_blocks):
    columns = diag_blocks.shape[1]
    width = diag_blocks.shape[2]
    panel_height = panel_blocks.shape[2]
    lower_rows = jnp.roll(next_rows, -1, axis=0)
    lower_panels = jnp.roll(panel_blocks, -1, axis=0)

    def row_work(index):
        upper = diag_rows[index]
        lower = lower_rows[index]
        target = routes[index].reshape(-1).astype(jnp.int32)

        def step(carry, item):
            gram_acc, cross_acc = carry
            block_x, block_y, where = item
            gram_acc = gram_acc.at[where].add(jnp.dot(block_x.astype(jnp.float32), block_x.T.astype(jnp.float32), preferred_element_type=jnp.float32))
            cross_acc = cross_acc.at[where].add(jnp.dot(block_y.astype(jnp.float32), block_x.T.astype(jnp.float32), preferred_element_type=jnp.float32))
            return ((gram_acc, cross_acc), None)
        empty_gram = jnp.zeros((columns, width, width), jnp.float32)
        empty_cross = jnp.zeros((columns, panel_height, width), jnp.float32)
        (gram_sum, cross_sum), unused = lax.scan(step, (empty_gram, empty_cross), (upper, lower, target))
        factor = jax.vmap(jnp.linalg.cholesky)(diag_blocks[index].astype(jnp.float32) + gram_sum)
        total = lower_panels[index].astype(jnp.float32) + cross_sum

        def solve_one(tri, rhs):
            return jax.scipy.linalg.solve_triangular(tri, rhs.T, lower=True).T
        solved = jax.vmap(solve_one)(factor, total)
        return (factor.astype(jnp.bfloat16), solved.astype(jnp.bfloat16))
    factors, panels = lax.map(row_work, jnp.arange(diag_blocks.shape[0], dtype=jnp.int32))
    return (factors, jnp.roll(panels, 1, axis=0))
```

```python
import numpy as np

import jax
import jax.numpy as jnp
from jax import lax
from jax.experimental import pallas as pl
from jax.experimental.pallas import tpu as pltpu
from jax.sharding import PartitionSpec as P


F32 = jnp.float32
BF16 = jnp.bfloat16
BS = 512
RB = 128
NB = BS // RB
SIDE = 4
STARTS = (0, 384, 640)
REST = 768


def place(x, y):
    return (x % SIDE) * SIDE + y % SIDE


def even(c):
    return (c // SIDE + c % SIDE) % 2 == 0


def shifted(c, along_x, d):
    return place(c // SIDE + d, c % SIDE) if along_x else place(c // SIDE, c % SIDE + d)


def first_hop(c, group, d):
    arrives_even = even(c) == (d % 2 == 0)
    return shifted(c, arrives_even == (group == 0), d)


def owners(c, group):
    if group == 0:
        return c, shifted(c, not even(c), 2)
    return shifted(c, even(c), 1), shifted(c, even(c), -1)


def order_table():
    rows = []
    for c in range(SIDE * SIDE):
        row = list(owners(c, 0) + owners(c, 1))
        for group in range(2):
            for d in (1, 2, 3):
                row += owners(first_hop(c, group, d), group)
        rows.append(row)
    return np.array(rows, np.int32)


def hop_pairs(group, d):
    return [(c, first_hop(c, group, d)) for c in range(SIDE * SIDE)]


def home_pairs(slot):
    return [(c, (owners(c, 0) + owners(c, 1))[slot]) for c in range(SIDE * SIDE)]


def pick_kernel(order, *refs):
    half = len(refs) // 2
    for src, dst in zip(refs[:half], refs[half:]):
        dst[...] = src[...]


def pick_pairs(order, blocks, bases):
    rows, width = blocks.shape[1:]

    def chosen(base):
        return pl.BlockSpec((1, rows, width), lambda i, o: (o[base + i], 0, 0))

    return pl.pallas_call(
        pick_kernel,
        out_shape=[jax.ShapeDtypeStruct((2, rows, width), BF16)] * len(bases),
        grid_spec=pltpu.PrefetchScalarGridSpec(
            num_scalar_prefetch=1,
            grid=(2,),
            in_specs=[chosen(b) for b in bases],
            out_specs=[pl.BlockSpec((1, rows, width), lambda i, o: (i, 0, 0))] * len(bases),
        ),
        cost_estimate=pl.CostEstimate(
            flops=0, bytes_accessed=len(bases) * 8 * rows * width, transcendentals=0
        ),
    )(order, *[blocks] * len(bases))


def xxt(a, b):
    return lax.dot_general(a, b, (((1,), (1,)), ((), ())), preferred_element_type=F32)


def first_part(blocks, outs_row):
    total = None
    for x in blocks:
        term = xxt(x[0, 0:RB, :], x[0])
        total = term if total is None else total + term
    outs_row[...] = total


def rest_part(blocks, out):
    for j in range(1, NB):
        total = None
        for x in blocks:
            term = xxt(x[0, RB * j : RB * j + RB, :], x[0, RB * j :, :])
            total = term if total is None else total + term
        start = STARTS[j - 1]
        out[:, start : start + BS - RB * j] = total


def sums_kernel(part):
    def kernel(order, *refs):
        own, group0, group1, outs = refs[0], refs[1:4], refs[4:7], refs[7:11]
        for slot in range(4):
            others = group0 if slot < 2 else group1

            @pl.when(pl.program_id(0) == slot)
            def _():
                part([own, *others], outs[slot])

    return kernel


def cross_kernel(order, *refs):
    own, group0, group1 = refs[0], refs[1:4], refs[4:7]
    yown, ygroup0, ygroup1, outs = refs[7], refs[8:11], refs[11:14], refs[14:18]
    for slot in range(4):
        xs = [own, *(group0 if slot < 2 else group1)]
        ys = [yown, *(ygroup0 if slot < 2 else ygroup1)]

        @pl.when(pl.program_id(0) == slot)
        def _():
            total = None
            for x, y in zip(xs, ys):
                term = xxt(y[0], x[0])
                total = term if total is None else total + term
            outs[slot][...] = total


def slot_specs(rows):
    own = pl.BlockSpec((1, rows, BS), lambda g, o: (o[g], 0, 0))
    low = pl.BlockSpec((1, rows, BS), lambda g, o: (jnp.minimum(g, 1), 0, 0))
    high = pl.BlockSpec((1, rows, BS), lambda g, o: (jnp.maximum(g - 2, 0), 0, 0))
    return [own] + [low] * 3 + [high] * 3


def partial_sums(kernel, order, arrays, in_specs, width, flops):
    return pl.pallas_call(
        kernel,
        out_shape=[jax.ShapeDtypeStruct((RB, width), F32)] * 4,
        grid_spec=pltpu.PrefetchScalarGridSpec(
            num_scalar_prefetch=1,
            grid=(4,),
            in_specs=in_specs,
            out_specs=[pl.BlockSpec((RB, width), lambda g, o: (0, 0))] * 4,
        ),
        cost_estimate=pl.CostEstimate(
            flops=flops, bytes_accessed=16 * BS * BS * 2, transcendentals=0
        ),
    )(order, *arrays)


def lane(v, k):
    return jnp.broadcast_to(v[:, k : k + 1], (8, 128))


def sublane(v, s):
    return jnp.broadcast_to(v[s : s + 1, :], (8, 128))


def factor_rows(w, u, tiles):
    at = lax.broadcasted_iota(jnp.int32, (8, 128), 0)
    here = [at == s for s in range(8)]
    span = [slice(128 * c, 128 * c + 128) for c in range(tiles)]
    for p in range(16):
        r0 = 8 * p
        rows = [w[r0 : r0 + 8, s] for s in span]
        cols = [lane(rows[0], r0 + s) for s in range(8)]
        done = [None] * tiles
        for s in range(0, 8, 2):
            e, f = cols[s], cols[s + 1]
            a, b, c = sublane(e, s), sublane(f, s), sublane(f, s + 1)
            inv = 1.0 / (a * c - b * b)
            ra = lax.rsqrt(a)
            bra = b * ra
            rc = lax.rsqrt(c - bra * bra)
            e = jnp.where(here[s], -1.0, jnp.where(here[s + 1], 0.0, e))
            f = jnp.where(here[s], 0.0, jnp.where(here[s + 1], -1.0, f))
            me = (c * e - b * f) * inv
            mf = (a * f - b * e) * inv
            pivot = jnp.logical_or(here[s], here[s + 1])
            for t in range(s + 2, 8):
                g, h = sublane(cols[t], s), sublane(cols[t], s + 1)
                cols[t] = jnp.where(pivot, 0.0, cols[t]) - me * g - mf * h
            for i in range(tiles):
                g, h = sublane(rows[i], s), sublane(rows[i], s + 1)
                ug = g * ra
                uh = (h - bra * ug) * rc
                base = ug if done[i] is None else jnp.where(here[s], ug, done[i])
                done[i] = jnp.where(here[s + 1], uh, base)
                rows[i] = jnp.where(pivot, 0.0, rows[i]) - me * g - mf * h
        for i in range(tiles):
            u[r0 : r0 + 8, span[i]] = done[i]
        for q in range(p + 1, 16):
            q0 = 8 * q
            lead = w[q0 : q0 + 8, span[0]]
            mult = [lane(lead, r0 + i) for i in range(8)]
            for i in range(tiles):
                t = [mult[k] * sublane(rows[i], k) for k in range(8)]
                total = ((t[0] + t[1]) + (t[2] + t[3])) + ((t[4] + t[5]) + (t[6] + t[7]))
                w[q0 : q0 + 8, span[i]] = w[q0 : q0 + 8, span[i]] - total


def exact(a, b, ca, cb):
    return lax.dot_general(
        a,
        b,
        (((ca,), (cb,)), ((), ())),
        precision=lax.Precision.HIGHEST,
        preferred_element_type=F32,
    )


def identity():
    r = lax.broadcasted_iota(jnp.int32, (RB, RB), 0)
    c = lax.broadcasted_iota(jnp.int32, (RB, RB), 1)
    return jnp.where(r == c, 1.0, 0.0)


def head_kernel(diag, own, got0, got1, got2, u, w):
    w[:, 0:BS] = diag[0:RB, :].astype(F32) + ((own[...] + got0[...]) + (got1[...] + got2[...]))
    w[:, BS:] = identity()
    factor_rows(w, u, NB + 1)


def tail_kernel(diag, own, got0, got1, got2, u0, u_out, acc, w, u):
    acc[...] = jnp.zeros_like(acc)
    for j in range(1, NB):
        n = BS - RB * j
        part = slice(STARTS[j - 1], STARTS[j - 1] + n)
        block = diag[RB * j : RB * j + RB, RB * j :].astype(F32)
        block = block + ((own[:, part] + got0[:, part]) + (got1[:, part] + got2[:, part]))
        acc[j - 1, :, 0:n] = block - exact(u0[:, RB * j : RB * j + RB], u0[:, RB * j : BS], 0, 0)
    eye = identity()

    def step(j, carry):
        w[:, 0 : BS - RB] = acc[j]
        w[:, BS - RB :] = eye
        factor_rows(w, u, NB)
        u_out[j] = u[...]
        for d in (1, 2):

            @pl.when(j + d < NB - 1)
            def _():
                n = (NB - 1 - d) * RB
                tile = u[:, RB * d : RB * d + RB]
                acc[j + d, :, 0:n] = acc[j + d, :, 0:n] - exact(tile, u[:, RB * d : BS - RB], 0, 0)

        return carry

    lax.fori_loop(0, NB - 1, step, 0)


def upper(u0, u, m, j):
    if m == 0:
        return u0[:, RB * j : RB * j + RB]
    return u[m - 1, :, RB * (j - m) : RB * (j - m) + RB]


def lower_inverse(u0, u, m):
    r = lax.broadcasted_iota(jnp.int32, (RB, RB), 0)
    c = lax.broadcasted_iota(jnp.int32, (RB, RB), 1)
    tile = u0[:, BS:] if m == 0 else u[m - 1, :, BS - RB :]
    return jnp.where(r >= c, tile, 0.0)


def solve_kernel(panel, own, got0, got1, got2, u0, u, out):
    total = panel[...].astype(F32) + ((own[...] + got0[...]) + (got1[...] + got2[...]))
    done = []
    for j in range(NB):
        x = total[:, RB * j : RB * j + RB]
        for m in range(j):
            x = x - exact(done[m], upper(u0, u, m, j), 1, 0)
        done.append(exact(x, lower_inverse(u0, u, j), 1, 1))
        out[:, RB * j : RB * j + RB] = done[j].astype(BF16)


def factor_kernel(u0, u, out):
    r = lax.broadcasted_iota(jnp.int32, (RB, RB), 0)
    c = lax.broadcasted_iota(jnp.int32, (RB, RB), 1)
    for i in range(NB):
        for j in range(NB):
            tile = (slice(RB * i, RB * i + RB), slice(RB * j, RB * j + RB))
            if j > i:
                out[tile] = jnp.zeros((RB, RB), BF16)
            else:
                block = upper(u0, u, j, i).T
                out[tile] = (jnp.where(r >= c, block, 0.0) if i == j else block).astype(BF16)


def dense(kernel, out_shape, args, scratch=(), flops=0):
    outs = out_shape if isinstance(out_shape, list) else [out_shape]
    size = sum(a.size * a.dtype.itemsize for a in (*args, *outs))
    return pl.pallas_call(
        kernel,
        out_shape=out_shape,
        in_specs=[pl.BlockSpec(memory_space=pltpu.VMEM)] * len(args),
        out_specs=jax.tree.map(lambda _: pl.BlockSpec(memory_space=pltpu.VMEM), out_shape),
        scratch_shapes=list(scratch),
        cost_estimate=pl.CostEstimate(flops=flops, bytes_accessed=size, transcendentals=0),
    )(*args)


def body(diag_rows, next_rows, routes, diag_blocks, panel_blocks):
    count = lax.axis_size("row")
    back = [(i, (i - 1) % count) for i in range(count)]
    ahead = [(i, (i + 1) % count) for i in range(count)]
    x_own = diag_rows[0]
    diag = diag_blocks[0, 0]

    wanted = jnp.asarray(order_table())[lax.axis_index("col")]
    hit = wanted[:, None] == routes[0, 0][None, :]
    order = jnp.sum(jnp.where(hit, jnp.arange(16, dtype=jnp.int32)[None, :], 0), axis=1)

    y_own = lax.ppermute(next_rows[0], "row", back)
    panel = lax.ppermute(panel_blocks[0, 0], "row", back)

    hops = [(g, d) for g in range(2) for d in (1, 2, 3)]
    base = {h: 4 + 2 * i for i, h in enumerate(hops)}
    x_got = {}
    for h in [(0, 1), (1, 1), (0, 3), (1, 3), (0, 2), (1, 2)]:
        (sent,) = pick_pairs(order, x_own, [base[h]])
        x_got[h] = lax.ppermute(sent, "col", hop_pairs(*h))
    y_sent = pick_pairs(order, y_own, [base[h] for h in hops])
    y_got = {h: lax.ppermute(s, "col", hop_pairs(*h)) for h, s in zip(hops, y_sent)}

    xs = [x_own] + [x_got[h] for h in hops]
    ys = [y_own] + [y_got[h] for h in hops]
    x_specs, y_specs = slot_specs(BS), slot_specs(RB)

    def home(parts):
        return [parts[0]] + [lax.ppermute(parts[s], "col", home_pairs(s)) for s in (1, 2, 3)]

    gram0 = home(partial_sums(sums_kernel(first_part), order, xs, x_specs, BS, 2 * 16 * RB * BS * BS))
    gram1 = home(partial_sums(sums_kernel(rest_part), order, xs, x_specs, REST, 3 * 16 * RB * BS * BS))
    cross = home(partial_sums(cross_kernel, order, xs + ys, x_specs + y_specs, BS, 2 * 16 * RB * BS * BS))

    tile = jax.ShapeDtypeStruct((RB, BS + RB), F32)
    u0 = dense(head_kernel, tile, (diag, *gram0), [pltpu.VMEM(tile.shape, F32)], flops=1 << 30)
    u = dense(
        tail_kernel,
        jax.ShapeDtypeStruct((NB - 1, RB, BS), F32),
        (diag, *gram1, u0),
        [
            pltpu.VMEM((NB - 1, RB, BS - RB), F32),
            pltpu.VMEM((RB, BS), F32),
            pltpu.VMEM((RB, BS), F32),
        ],
        flops=3 << 30,
    )
    solved = dense(
        solve_kernel, jax.ShapeDtypeStruct((RB, BS), BF16), (panel, *cross, u0, u), flops=1 << 28
    )
    panel_out = lax.ppermute(solved, "row", ahead)
    factor = dense(factor_kernel, jax.ShapeDtypeStruct((BS, BS), BF16), (u0, u), flops=1 << 28)
    return factor[None, None], panel_out[None, None]


def solution(mesh):
    blocks = P("row", "col", None, None)
    return jax.shard_map(
        body,
        mesh=mesh,
        in_specs=(blocks, blocks, P("row", "col", None), blocks, blocks),
        out_specs=(blocks, blocks),
        check_vma=False,
    )
```
